256 devices in a mesh: dp: 32 (over x, y, core), seq: 8 (over z).
Axes of the slice: x: 4, y: 4, z: 8, core: 2. Of those that a mesh axis runs over, the one named last changes fastest.
Arguments:
- tokens: bfloat16 [32, 2048, 5120], P('dp', 'seq'), may hold values from -6 to 6
- queries: bfloat16 [32, 2048, 2560], P('dp', 'seq'), may hold values from -400 to 400
- cotangent: bfloat16 [32, 2048, 2560], P('dp', 'seq'), may hold values from -6 to 6
- kv_weight: bfloat16 [5120, 1024], P('dp'), may hold values from -0.078125 to 0.078125
- active: int32 [32, 8], P('dp'), may hold values from 0 to 15, as said below
Outputs:
- query_grads: bfloat16 [32, 2048, 2560], P('dp', 'seq')
- token_grads: bfloat16 [32, 2048, 5120], P('dp', 'seq')
- weight_grad: float32 [5120, 1024], P('dp', 'seq')
The draws below stay inside these ranges and needn't reach their ends.
Inputs may be any that keep to these rules, and one draw needn't show every extreme that they name: active[p] lists 8 different blocks of sequence p in increasing order; blocks 0 and 15 are always among them.
All inputs are finite; a program needn't handle non-finite values.
Results may differ from the reference program's by a relative error of at most 0.019.
The reference program's roundings to bfloat16 on the way count: a program that leaves them out, or rounds other values in their place, can miss the bound.
Values may be sent and summed in bfloat16 or wider, within the bound.
A program may use at most 128 MiB of HBM per device.

```python
import math
import jax
import jax.numpy as jnp
from jax import lax

D = 5120
HEAD_SIZE = 128
QUERY_HEADS = 20
KEY_VALUE_HEADS = 4
BLK = 128
TOK_DEV = 256
SEQLEN = 2048
NBLK = 16
NACT = 8
QW = 2560
KVW = 1024
N_DP = 32
N_SEQ = 8


def draw_queries(key, part):
    key_base, key_scale = jax.random.split(key)
    base = jax.random.normal(key_base, (N_DP, SEQLEN, QUERY_HEADS * HEAD_SIZE), jnp.float32)
    spread_log = jax.random.uniform(key_scale, (N_DP, SEQLEN, 1), jnp.float32, math.log(0.5), math.log(2.0))
    return jnp.clip(base * jnp.exp(spread_log), -400.0, 400.0).astype(jnp.bfloat16)


def draw_active(key, part):

    def one_row(row_key):
        inner = jax.random.permutation(row_key, NBLK - 2)[:NACT - 2] + 1
        chosen = jnp.concatenate([jnp.zeros((1,), jnp.int32), inner.astype(jnp.int32), jnp.full((1,), NBLK - 1, jnp.int32)])
        return jnp.sort(chosen)
    return jax.vmap(one_row)(jax.random.split(key, N_DP))


def level_of(key, shape, shards, smallest, top_value):
    factor_of, own = 1.0, jax.random.fold_in(key, 6)
    for axis_at, parts in shards:
        heights = jnp.exp(jax.random.uniform(jax.random.fold_in(own, axis_at), (parts,), jnp.float32, smallest / len(shards), top_value / len(shards)))
        factor_of = factor_of * jnp.repeat(heights, shape[axis_at] // parts).reshape([-1 if axis == axis_at else 1 for axis in range(len(shape))])
    return factor_of


def scatter_about(key, dims, deviation, limit, cuts=(), kind=jnp.bfloat16):
    gain = level_of(key, dims, cuts, -0.22, 0.18) if cuts else 1.0
    drawn = jax.random.normal(key, dims, jnp.float32) * deviation * gain
    return jnp.minimum(jnp.maximum(drawn, -limit), limit).astype(kind)


def setup_inputs(seed: int = 0) -> dict:
    key_of = jax.random.split(jax.random.key(seed), 6)
    return {
        "tokens": scatter_about(key_of[0], (N_DP, SEQLEN, D), 1.0, 6.0, ((0, 32), (1, 8))),
        "queries": draw_queries(jax.random.fold_in(key_of[5], 71), 0),
        "cotangent": scatter_about(key_of[2], (N_DP, SEQLEN, QW), 1.0, 6.0, ((0, 32), (1, 8))),
        "kv_weight": scatter_about(key_of[3], (D, KVW), D ** -0.5, 0.078125, ((0, 32),)),
        "active": draw_active(jax.random.fold_in(key_of[5], 71), 0),
    }


def lower_precision(value):
    return lax.optimization_barrier(value.astype(jnp.bfloat16))

def reference(tokens, queries, cotangent, kv_weight, active):
    head_group = QUERY_HEADS // KEY_VALUE_HEADS
    routed_count = NACT * BLK
    scale = 1.0 / math.sqrt(HEAD_SIZE)

    def one_sequence(grad_total, pieces):
        tokens_p, query_parts, output_cotangent_parts, block_ids = pieces
        token_positions = (block_ids[:, None] * BLK + jnp.arange(BLK, dtype=jnp.int32)[None, :]).reshape(-1).astype(jnp.int32)
        x_act = tokens_p[token_positions]
        keyval = lower_precision(jnp.dot(x_act, kv_weight, preferred_element_type=jnp.float32))
        key_value_wide = keyval.astype(jnp.float32)
        key_matrix = key_value_wide[:, :KEY_VALUE_HEADS * HEAD_SIZE].reshape(routed_count, KEY_VALUE_HEADS, HEAD_SIZE)
        value_matrix = key_value_wide[:, KEY_VALUE_HEADS * HEAD_SIZE:].reshape(routed_count, KEY_VALUE_HEADS, HEAD_SIZE)
        active_query = query_parts[token_positions].astype(jnp.float32).reshape(routed_count, KEY_VALUE_HEADS, head_group, HEAD_SIZE)
        active_gradient = output_cotangent_parts[token_positions].astype(jnp.float32).reshape(routed_count, KEY_VALUE_HEADS, head_group, HEAD_SIZE)
        scores = jnp.einsum('ikgd,jkd->kgij', active_query, key_matrix) * scale
        causal = jnp.arange(routed_count)[None, :] <= jnp.arange(routed_count)[:, None]
        scores = jnp.where(causal, scores, -1e+30)
        row_max = lax.optimization_barrier(jnp.max(scores, axis=-1, keepdims=True))
        exponent = jnp.exp(scores - row_max)
        probs = exponent / lax.optimization_barrier(jnp.sum(exponent, axis=-1, keepdims=True))
        probs_low = lower_precision(probs).astype(jnp.float32)
        attended = jnp.einsum('kgij,jkd->ikgd', probs_low, value_matrix)
        row_delta = jnp.einsum('ikgd,ikgd->kgi', active_gradient, attended)
        dprobs = jnp.einsum('ikgd,jkd->kgij', active_gradient, value_matrix)
        dscores = lower_precision(probs * (dprobs - row_delta[..., None]) * scale).astype(jnp.float32)
        query_grad = jnp.einsum('kgij,jkd->ikgd', dscores, key_matrix).astype(jnp.bfloat16).reshape(routed_count, QW)
        key_gradient = jnp.einsum('kgij,ikgd->jkd', dscores, active_query)
        value_gradient = jnp.einsum('kgij,ikgd->jkd', probs_low, active_gradient)
        key_value_gradient = lower_precision(jnp.concatenate([key_gradient.reshape(routed_count, KEY_VALUE_HEADS * HEAD_SIZE), value_gradient.reshape(routed_count, KEY_VALUE_HEADS * HEAD_SIZE)], axis=1))
        token_grad = lax.dot_general(key_value_gradient, kv_weight, (((1,), (1,)), ((), ())), preferred_element_type=jnp.float32).astype(jnp.bfloat16)
        full_query = jnp.zeros((SEQLEN, QW), jnp.bfloat16).at[token_positions].set(query_grad)
        full_token = jnp.zeros((SEQLEN, D), jnp.bfloat16).at[token_positions].set(token_grad)
        full_kv = jnp.zeros((SEQLEN, KVW), jnp.bfloat16).at[token_positions].set(key_value_gradient)
        terms = jnp.einsum('std,stc->sdc', tokens_p.reshape(N_SEQ, TOK_DEV, D).astype(jnp.float32), full_kv.reshape(N_SEQ, TOK_DEV, KVW).astype(jnp.float32))
        grad_total = grad_total + lax.optimization_barrier(jnp.sum(lower_precision(terms).astype(jnp.float32), axis=0))
        return (grad_total, (full_query, full_token))
    weight_grad, outputs = lax.scan(one_sequence, jnp.zeros((D, KVW), jnp.float32), (tokens, queries, cotangent, active))
    return (outputs[0], outputs[1], weight_grad)
```

```python
import math

import jax
import jax.numpy as jnp
from jax import lax
from jax.experimental import pallas as pl
from jax.experimental.pallas import tpu as pltpu
from jax.sharding import PartitionSpec as P

HEAD = 128
BLK = 128
NBLK = 16
NACT = 8
KVH = 4
GRP = 5
HALF = 64
ROWS = GRP * HALF
BF = jnp.bfloat16
F32 = jnp.float32
MESH = pl.DeviceIdType.MESH
VM = pl.BlockSpec(memory_space=pltpu.VMEM)
NT = (((1,), (1,)), ((), ()))


def attention_kernel(act, q_ref, g_ref, kv_ref, qg_ref, dkv_ref, kc, vc, sc, dp, pb, ds, dkt, dvt):
    scale = 1.0 / math.sqrt(HEAD)
    half = act[NACT]
    for j in range(NACT):
        block = kv_ref[act[j]]
        kc[j * BLK : (j + 1) * BLK, :] = block[:, :HEAD]
        vc[j * BLK : (j + 1) * BLK, :] = block[:, HEAD:]
    qg_ref[...] = jnp.zeros_like(qg_ref)
    dkv_ref[...] = jnp.zeros_like(dkv_ref)
    step = 32
    for a in reversed(range(NACT)):
        n = (a + 1) * BLK
        b = act[a]
        q5 = jnp.concatenate([q_ref[b, :, i * HEAD : (i + 1) * HEAD] for i in range(GRP)], axis=0)
        g5 = jnp.concatenate([g_ref[b, :, i * HEAD : (i + 1) * HEAD] for i in range(GRP)], axis=0)
        sc[:, :n] = lax.dot_general(q5, kc[:n, :], NT, preferred_element_type=F32)
        dp[:, :n] = lax.dot_general(g5, vc[:n, :], NT, preferred_element_type=F32)

        def softmax(i, carry):
            rows = pl.ds(pl.multiple_of(i * step, step), step)
            s = sc[rows, :n] * scale
            pos = half * HALF + lax.rem(i, HALF // step) * step + lax.broadcasted_iota(jnp.int32, (step, BLK), 0)
            col = lax.broadcasted_iota(jnp.int32, (step, BLK), 1)
            last = jnp.where(col <= pos, s[:, n - BLK :], -1e30)
            s = last if a == 0 else jnp.concatenate([s[:, : n - BLK], last], axis=1)
            e = jnp.exp(s - jnp.max(s, axis=-1, keepdims=True))
            p = e / jnp.sum(e, axis=-1, keepdims=True)
            low = p.astype(BF)
            d = dp[rows, :n]
            delta = jnp.sum(low.astype(F32) * d, axis=-1, keepdims=True)
            pb[rows, :n] = low
            ds[rows, :n] = (p * (d - delta) * scale).astype(BF)
            return carry

        lax.fori_loop(0, ROWS // step, softmax, 0)
        dq = jnp.dot(ds[:, :n], kc[:n, :], preferred_element_type=F32).astype(BF)
        for i in range(GRP):
            qg_ref[b, :, i * HEAD : (i + 1) * HEAD] = dq[i * HALF : (i + 1) * HALF, :]
        dk = jnp.dot(q5.T, ds[:, :n], preferred_element_type=F32)
        dv = jnp.dot(g5.T, pb[:, :n], preferred_element_type=F32)
        if a == NACT - 1:
            dkt[...] = dk
            dvt[...] = dv
        else:
            dkt[:, :n] += dk
            dvt[:, :n] += dv
    for j in range(NACT):
        b = act[j]
        dkv_ref[b, :, :HEAD] = dkt[:, j * BLK : (j + 1) * BLK].T.astype(BF)
        dkv_ref[b, :, HEAD:] = dvt[:, j * BLK : (j + 1) * BLK].T.astype(BF)


def attention(act, q, g, kv):
    n = NACT * BLK
    return pl.pallas_call(
        attention_kernel,
        out_shape=(jax.ShapeDtypeStruct(q.shape, BF), jax.ShapeDtypeStruct(kv.shape, BF)),
        in_specs=[pl.BlockSpec(memory_space=pltpu.SMEM), VM, VM, VM],
        out_specs=(VM, VM),
        scratch_shapes=[
            pltpu.VMEM((n, HEAD), BF),
            pltpu.VMEM((n, HEAD), BF),
            pltpu.VMEM((ROWS, n), F32),
            pltpu.VMEM((ROWS, n), F32),
            pltpu.VMEM((ROWS, n), BF),
            pltpu.VMEM((ROWS, n), BF),
            pltpu.VMEM((HEAD, n), F32),
            pltpu.VMEM((HEAD, n), F32),
        ],
        name="attention",
    )(act, q, g, kv)


def grad_kernel(x_ref, dk_ref, out_ref, kvb_ref, kv2, total, s1, r1, s2, r2, s3, r3, mine, ssem, rsem):
    me = lax.axis_index("dp")
    z = lax.axis_index("seq")
    c = lax.rem(me, 2)
    cy = lax.rem(me // 2, 4)
    cx = me // 8
    f = cx + (cy - cx) * c
    s = cy + (cx - cy) * c

    def device(ff, ss):
        return ff * (8 - 6 * c) + ss * (2 + 6 * c) + c

    partner = me + 1 - 2 * c
    f_right, f_left, f_far = lax.rem(f + 1, 4), lax.rem(f + 3, 4), lax.rem(f + 2, 4)
    s_right, s_left, s_far = lax.rem(s + 1, 4), lax.rem(s + 3, 4), lax.rem(s + 2, 4)
    right1, left1 = device(f_right, s), device(f_left, s)
    right2, left2 = device(f, s_right), device(f, s_left)

    barrier = pltpu.get_barrier_semaphore()
    for peer in (partner, right1, left1, right2, left2):
        pl.semaphore_signal(barrier, inc=1, device_id=(peer, z), device_id_type=MESH)
    for k in range(1, 8):
        pl.semaphore_signal(barrier, inc=1, device_id=(me, lax.rem(z + k, 8)), device_id_type=MESH)
    for h in range(KVH):
        for part in range(2):
            lanes = slice(part * HEAD, (part + 1) * HEAD)
            both = dk_ref[2 * h, :, lanes].astype(F32) + dk_ref[2 * h + 1, :, lanes].astype(F32)
            kv2[0:256, (part * KVH + h) * HEAD : (part * KVH + h + 1) * HEAD] = both.astype(BF)
    pl.semaphore_wait(barrier, 12)

    def send(index, src, dst, dev, seq):
        copy = pltpu.make_async_remote_copy(
            src_ref=src,
            dst_ref=dst,
            send_sem=ssem.at[index],
            recv_sem=rsem.at[index],
            device_id=(dev, seq),
            device_id_type=MESH,
        )
        copy.start()
        return copy

    swap = send(0, kv2.at[0:256], kv2.at[256:512], partner, z)
    kvb_ref[...] = kv2[0:256, :]
    swap.wait()

    def product(ff, part):
        return jnp.dot(x_ref[ff, part * 320 : (part + 1) * 320, :], kv2[...], preferred_element_type=F32)

    s1[0] = product(f_far, 0).astype(BF)
    far_r = send(1, s1.at[0], r1.at[0], right1, z)
    s1[1] = product(f_far, 1).astype(BF)
    far_l = send(2, s1.at[1], r1.at[1], left1, z)
    s1[2] = product(f_right, 1).astype(BF)
    own_r = send(3, s1.at[2], r1.at[2], right1, z)
    s1[3] = product(f_left, 0).astype(BF)
    own_l = send(4, s1.at[3], r1.at[3], left1, z)
    total[0:2] = product(f_right, 0).reshape(2, 160, 1024)
    far_r.wait_recv()
    s1[4] = (total[0:2].reshape(320, 1024) + r1[0].astype(F32)).astype(BF)
    sum_r = send(5, s1.at[4], r1.at[4], right1, z)
    total[2:4] = product(f_left, 1).reshape(2, 160, 1024)
    far_l.wait_recv()
    s1[5] = (total[2:4].reshape(320, 1024) + r1[1].astype(F32)).astype(BF)
    sum_l = send(6, s1.at[5], r1.at[5], left1, z)
    total[0:2] = product(f, 0).reshape(2, 160, 1024)
    total[2:4] = product(f, 1).reshape(2, 160, 1024)
    own_r.wait_recv()
    own_l.wait_recv()
    total[0:2] += r1[3].astype(F32).reshape(2, 160, 1024)
    total[2:4] += r1[2].astype(F32).reshape(2, 160, 1024)
    sum_r.wait_recv()
    total[0:2] += r1[4].astype(F32).reshape(2, 160, 1024)
    sum_l.wait_recv()
    total[2:4] += r1[5].astype(F32).reshape(2, 160, 1024)

    s2[0] = total[s_far, 0:80, :].astype(BF)
    far_r2 = send(7, s2.at[0], r2.at[0], right2, z)
    s2[1] = total[s_far, 80:160, :].astype(BF)
    far_l2 = send(8, s2.at[1], r2.at[1], left2, z)
    s2[2] = total[s_right, 80:160, :].astype(BF)
    own_r2 = send(9, s2.at[2], r2.at[2], right2, z)
    s2[3] = total[s_left, 0:80, :].astype(BF)
    own_l2 = send(10, s2.at[3], r2.at[3], left2, z)
    far_r2.wait_recv()
    s2[4] = (total[s_right, 0:80, :] + r2[0].astype(F32)).astype(BF)
    sum_r2 = send(11, s2.at[4], r2.at[4], right2, z)
    far_l2.wait_recv()
    s2[5] = (total[s_left, 80:160, :] + r2[1].astype(F32)).astype(BF)
    sum_l2 = send(12, s2.at[5], r2.at[5], left2, z)
    own_r2.wait_recv()
    own_l2.wait_recv()
    sum_r2.wait_recv()
    top = total[s, 0:80, :] + r2[3].astype(F32) + r2[4].astype(F32)
    sum_l2.wait_recv()
    low = total[s, 80:160, :] + r2[2].astype(F32) + r2[5].astype(F32)
    for t in range(8):
        lanes = slice(t * 128, (t + 1) * 128)
        mine[t, 0:80, :] = top[:, lanes]
        mine[t, 80:160, :] = low[:, lanes]
        s3[t, 0:80, :] = top[:, lanes].astype(BF)
        s3[t, 80:160, :] = low[:, lanes].astype(BF)
    ends = []
    for k in range(1, 8):
        t = lax.rem(z + k, 8)
        ends.append(send(12 + k, s3.at[t], r3.at[k - 1], me, t))
    out = mine[z]
    for k in range(1, 8):
        ends[k - 1].wait_recv()
        out = out + r3[k - 1].astype(F32)
    out_ref[...] = out
    for copy in [far_r, far_l, own_r, own_l, sum_r, sum_l, far_r2, far_l2, own_r2, own_l2, sum_r2, sum_l2] + ends:
        copy.wait_send()


def weight_gradient(x, dk):
    return pl.pallas_call(
        grad_kernel,
        out_shape=(jax.ShapeDtypeStruct((160, 128), F32), jax.ShapeDtypeStruct((256, 1024), BF)),
        in_specs=[VM, VM],
        out_specs=(VM, VM),
        scratch_shapes=[
            pltpu.VMEM((512, 1024), BF),
            pltpu.VMEM((4, 160, 1024), F32),
            pltpu.VMEM((6, 320, 1024), BF),
            pltpu.VMEM((6, 320, 1024), BF),
            pltpu.VMEM((6, 80, 1024), BF),
            pltpu.VMEM((6, 80, 1024), BF),
            pltpu.VMEM((8, 160, 128), BF),
            pltpu.VMEM((7, 160, 128), BF),
            pltpu.VMEM((8, 160, 128), F32),
            pltpu.SemaphoreType.DMA((20,)),
            pltpu.SemaphoreType.DMA((20,)),
        ],
        compiler_params=pltpu.CompilerParams(collective_id=0, has_side_effects=True),
        cost_estimate=pl.CostEstimate(flops=5_400_000_000, bytes_accessed=60_000_000, transcendentals=0),
        name="weight_gradient",
    )(x, dk)


def body(tokens, queries, cotangent, kv_weight, active):
    dp = lax.axis_index("dp")
    z = lax.axis_index("seq")
    core = lax.rem(dp, 2)

    def spread(v):
        v = v.reshape(2, 2, HALF, KVH, GRP * HEAD).transpose(3, 1, 0, 2, 4)
        return v.reshape(8, 2, HALF, GRP * HEAD)

    def swap(v):
        return lax.all_to_all(v, "seq", split_axis=0, concat_axis=0, tiled=True)

    x = tokens[0]
    q_in = swap(spread(queries[0]))
    g_in = swap(spread(cotangent[0]))
    weight = lax.all_gather(kv_weight, "dp", axis=0, tiled=True)

    x_t = x.T.reshape(4, 4, 2, 160, 256)

    def half_of(which):
        return jnp.where(which == 0, x_t[:, :, 0], x_t[:, :, 1].transpose(1, 0, 2, 3)).reshape(4, 640, 256)

    x_mine = half_of(core)
    x_theirs = lax.ppermute(half_of(1 - core), "dp", [(i, i ^ 1) for i in range(32)])
    x_cat = jnp.concatenate([x_mine, x_theirs], axis=2)

    q_in, g_in, weight, x_cat, x = lax.optimization_barrier((q_in, g_in, weight, x_cat, x))
    keyval = jnp.dot(x, weight, preferred_element_type=F32).astype(BF)
    kv_out = keyval.reshape(256, 2, KVH, HEAD).transpose(2, 0, 1, 3).reshape(KVH, 1, 256, 256)
    kv_out = jnp.broadcast_to(kv_out, (KVH, 2, 256, 256)).reshape(8, 256, 256)
    kv_in = swap(kv_out).reshape(NBLK, BLK, 256)
    act = jnp.concatenate([active[0], lax.rem(z, 2)[None].astype(jnp.int32)])
    qg, dkv = attention(act, q_in.reshape(NBLK, HALF, GRP * HEAD), g_in.reshape(NBLK, HALF, GRP * HEAD), kv_in)
    dk = swap(dkv.reshape(8, 256, 256))
    q_back = swap(qg.reshape(8, 2, HALF, GRP * HEAD))
    part, kv_back = weight_gradient(x_cat, dk)
    q_back = q_back.reshape(KVH, 2, 2, HALF, GRP * HEAD).transpose(2, 1, 3, 0, 4).reshape(256, 2560)
    token_grad = lax.dot_general(kv_back, weight, NT, preferred_element_type=F32).astype(BF)
    return (q_back[None], token_grad[None], part)


def solution(mesh):
    in_specs = (
        P("dp", "seq", None),
        P("dp", "seq", None),
        P("dp", "seq", None),
        P("dp", None),
        P("dp", None),
    )
    out_specs = (P("dp", "seq", None), P("dp", "seq", None), P("dp", "seq"))
    return jax.shard_map(body, mesh=mesh, in_specs=in_specs, out_specs=out_specs, check_vma=False)
```

```python
import math

import jax
import jax.numpy as jnp
from jax import lax
from jax.experimental import pallas as pl
from jax.experimental.pallas import tpu as pltpu
from jax.sharding import PartitionSpec as P

HEAD = 128
BLK = 128
NBLK = 16
NACT = 8
KVH = 4
GRP = 5
HALF = 64
ROWS = GRP * HALF
BF = jnp.bfloat16
F32 = jnp.float32
MESH = pl.DeviceIdType.MESH
VM = pl.BlockSpec(memory_space=pltpu.VMEM)
NT = (((1,), (1,)), ((), ()))


def attention_kernel(act, q_ref, g_ref, kv_ref, qg_ref, dkv_ref, kc, vc, sc, dp, pb, ds, dkt, dvt):
    scale = 1.0 / math.sqrt(HEAD)
    half = act[NACT]
    for j in range(NACT):
        block = kv_ref[act[j]]
        kc[j * BLK : (j + 1) * BLK, :] = block[:, :HEAD]
        vc[j * BLK : (j + 1) * BLK, :] = block[:, HEAD:]
    qg_ref[...] = jnp.zeros_like(qg_ref)
    step = 32
    for a in reversed(range(NACT)):
        n = (a + 1) * BLK
        b = act[a]
        q5 = jnp.concatenate([q_ref[b, :, i * HEAD : (i + 1) * HEAD] for i in range(GRP)], axis=0)
        g5 = jnp.concatenate([g_ref[b, :, i * HEAD : (i + 1) * HEAD] for i in range(GRP)], axis=0)
        sc[:, :n] = lax.dot_general(q5, kc[:n, :], NT, preferred_element_type=F32)
        dp[:, :n] = lax.dot_general(g5, vc[:n, :], NT, preferred_element_type=F32)

        def softmax(i, carry):
            rows = pl.ds(pl.multiple_of(i * step, step), step)
            s = sc[rows, :n] * scale
            pos = half * HALF + lax.rem(i, HALF // step) * step + lax.broadcasted_iota(jnp.int32, (step, BLK), 0)
            col = lax.broadcasted_iota(jnp.int32, (step, BLK), 1)
            last = jnp.where(col <= pos, s[:, n - BLK :], -1e30)
            s = last if a == 0 else jnp.concatenate([s[:, : n - BLK], last], axis=1)
            e = jnp.exp(s - jnp.max(s, axis=-1, keepdims=True))
            p = e / jnp.sum(e, axis=-1, keepdims=True)
            low = p.astype(BF)
            d = dp[rows, :n]
            delta = jnp.sum(low.astype(F32) * d, axis=-1, keepdims=True)
            pb[rows, :n] = low
            ds[rows, :n] = (p * (d - delta) * scale).astype(BF)
            return carry

        lax.fori_loop(0, ROWS // step, softmax, 0)
        dq = jnp.dot(ds[:, :n], kc[:n, :], preferred_element_type=F32).astype(BF)
        for i in range(GRP):
            qg_ref[b, :, i * HEAD : (i + 1) * HEAD] = dq[i * HALF : (i + 1) * HALF, :]
        dk = jnp.dot(q5.T, ds[:, :n], preferred_element_type=F32)
        dv = jnp.dot(g5.T, pb[:, :n], preferred_element_type=F32)
        if a == NACT - 1:
            dkt[...] = dk
            dvt[...] = dv
        else:
            dkt[:, :n] += dk
            dvt[:, :n] += dv
    for j in range(NACT):
        dkv_ref[0, j] = dkt[:, j * BLK : (j + 1) * BLK].T
        dkv_ref[1, j] = dvt[:, j * BLK : (j + 1) * BLK].T


def attention(act, q, g, kv):
    n = NACT * BLK
    return pl.pallas_call(
        attention_kernel,
        out_shape=(jax.ShapeDtypeStruct(q.shape, BF), jax.ShapeDtypeStruct((2, NACT, BLK, HEAD), F32)),
        in_specs=[pl.BlockSpec(memory_space=pltpu.SMEM), VM, VM, VM],
        out_specs=(VM, VM),
        scratch_shapes=[
            pltpu.VMEM((n, HEAD), BF),
            pltpu.VMEM((n, HEAD), BF),
            pltpu.VMEM((ROWS, n), F32),
            pltpu.VMEM((ROWS, n), F32),
            pltpu.VMEM((ROWS, n), BF),
            pltpu.VMEM((ROWS, n), BF),
            pltpu.VMEM((HEAD, n), F32),
            pltpu.VMEM((HEAD, n), F32),
        ],
        name="attention",
    )(act, q, g, kv)


def ring_places():
    me = lax.axis_index("dp")
    c = lax.rem(me, 2)
    cy = lax.rem(me // 2, 4)
    cx = me // 8
    return me, c, cx + (cy - cx) * c, cy + (cx - cy) * c


def greet(peers, me, z):
    barrier = pltpu.get_barrier_semaphore()
    for peer in peers:
        pl.semaphore_signal(barrier, inc=1, device_id=(peer, z), device_id_type=MESH)
    for k in range(1, 8):
        pl.semaphore_signal(barrier, inc=1, device_id=(me, lax.rem(z + k, 8)), device_id_type=MESH)
    return barrier


def remote(src, dst, ssem, rsem, dev, seq):
    copy = pltpu.make_async_remote_copy(
        src_ref=src, dst_ref=dst, send_sem=ssem, recv_sem=rsem, device_id=(dev, seq), device_id_type=MESH
    )
    copy.start()
    return copy


def local(src, dst, sem):
    copy = pltpu.make_async_copy(src, dst, sem)
    copy.start()
    return copy


def seq_lanes(t):
    return pl.ds(pl.multiple_of((t // 2) * (GRP * HEAD), 128), GRP * HEAD)


def seq_rows(t):
    return pl.ds(pl.multiple_of(lax.rem(t, 2) * HALF, HALF), HALF)


def gather_kernel(q_ref, g_ref, w_in, x_ref, q_out, g_out, kv_out, w_out, w, kvb, acc, zs, zr, ws, wr, ls):
    z = lax.axis_index("seq")
    me, c, f, s = ring_places()

    def device(ff, ss):
        return ff * (8 - 6 * c) + ss * (2 + 6 * c) + c

    partner = me + 1 - 2 * c
    f_right, f_left, f_far = lax.rem(f + 1, 4), lax.rem(f + 3, 4), lax.rem(f + 2, 4)
    s_right, s_left, s_far = lax.rem(s + 1, 4), lax.rem(s + 3, 4), lax.rem(s + 2, 4)
    right1, left1 = device(f_right, s), device(f_left, s)
    right2, left2 = device(f, s_right), device(f, s_left)
    barrier = greet((partner, right1, left1, right2, left2), me, z)
    locals_ = [local(w_in, w.at[me], ls.at[0])]
    locals_.append(local(q_ref.at[:, seq_rows(z), seq_lanes(z)], q_out.at[z], ls.at[1]))
    locals_.append(local(g_ref.at[:, seq_rows(z), seq_lanes(z)], g_out.at[z], ls.at[2]))
    locals_[0].wait()
    pl.semaphore_wait(barrier, 12)

    count = [0]
    rings = []

    def push(src, dev):
        n = count[0]
        count[0] += 1
        copy = remote(src, src, ws.at[n], wr.at[n], dev, z)
        rings.append(copy)
        return copy

    def half(i, p):
        return w.at[i, p * 80 : (p + 1) * 80]

    a_right, a_left = push(w.at[me], right1), push(w.at[me], left1)
    second = [(f, push(w.at[me], right2), push(w.at[me], left2))]
    chip = [push(w.at[me], partner)]
    ends = []
    for ref, out, base in ((q_ref, q_out, 0), (g_ref, g_out, 7)):
        for k in (1, 7, 2, 6, 3, 5, 4):
            t = lax.rem(z + k, 8)
            ends.append(
                remote(ref.at[:, seq_rows(t), seq_lanes(t)], out.at[z], zs.at[base + k - 1], zr.at[base + k - 1], me, t)
            )

    def ready(ff, ss):
        i = device(ff, ss)
        chip.append(push(w.at[i], partner))
        return i

    a_right.wait_recv()
    i = device(f_left, s)
    far_a = push(half(i, 0), right1)
    second.append((f_left, push(w.at[i], right2), push(w.at[i], left2)))
    ready(f_left, s)
    a_left.wait_recv()
    i = device(f_right, s)
    far_b = push(half(i, 1), left1)
    second.append((f_right, push(w.at[i], right2), push(w.at[i], left2)))
    ready(f_right, s)
    thirds = []

    def forward(entry):
        ff, to_right, to_left = entry
        to_right.wait_recv()
        i = ready(ff, s_left)
        one = push(half(i, 0), right2)
        to_left.wait_recv()
        i = ready(ff, s_right)
        thirds.append((ff, one, push(half(i, 1), left2)))

    forward(second[0])
    far_a.wait_recv()
    far_b.wait_recv()
    i = ready(f_far, s)
    second.append((f_far, push(w.at[i], right2), push(w.at[i], left2)))
    for entry in second[1:]:
        forward(entry)
    for ff, one, two in thirds:
        one.wait_recv()
        two.wait_recv()
        ready(ff, s_far)
    for copy in chip:
        copy.wait_recv()
    locals_.append(local(w, w_out, ls.at[3]))

    def tile(j):
        block = w[4 * j : 4 * j + 4].reshape(640, 1024)
        return jnp.dot(x_ref[:, j * 640 : (j + 1) * 640], block, preferred_element_type=F32)

    acc[...] = tile(0)
    for j in range(1, 8):
        acc[...] += tile(j)
    for h in range(KVH):
        kvb[h, :, :HEAD] = acc[:, h * HEAD : (h + 1) * HEAD].astype(BF)
        kvb[h, :, HEAD:] = acc[:, (KVH + h) * HEAD : (KVH + h + 1) * HEAD].astype(BF)
    locals_.append(local(kvb.at[z // 2], kv_out.at[z], ls.at[4]))
    for k in (1, 7, 2, 6, 3, 5, 4):
        t = lax.rem(z + k, 8)
        ends.append(remote(kvb.at[t // 2], kv_out.at[z], zs.at[13 + k], zr.at[13 + k], me, t))
    for copy in rings:
        copy.wait_send()
    for copy in ends:
        copy.wait()
    for copy in locals_[1:]:
        copy.wait()


ANY = pl.BlockSpec(memory_space=pl.ANY)


def gather(q, g, w, x):
    piece = jax.ShapeDtypeStruct((8, 2, HALF, GRP * HEAD), BF)
    return pl.pallas_call(
        gather_kernel,
        out_shape=(
            piece,
            piece,
            jax.ShapeDtypeStruct((8, 256, 256), BF),
            jax.ShapeDtypeStruct((32, 160, 1024), BF),
        ),
        in_specs=[ANY, ANY, ANY, VM],
        out_specs=(ANY, ANY, ANY, ANY),
        scratch_shapes=[
            pltpu.VMEM((32, 160, 1024), BF),
            pltpu.VMEM((4, 256, 256), BF),
            pltpu.VMEM((256, 1024), F32),
            pltpu.SemaphoreType.DMA((21,)),
            pltpu.SemaphoreType.DMA((21,)),
            pltpu.SemaphoreType.DMA((36,)),
            pltpu.SemaphoreType.DMA((36,)),
            pltpu.SemaphoreType.DMA((5,)),
        ],
        compiler_params=pltpu.CompilerParams(collective_id=1, has_side_effects=True),
        name="gather",
    )(q, g, w, x)


def grad_kernel(
    inv, x_ref, dk_ref, qg_ref, out_ref, kvb_ref, q_out, kv2, pair, summed, pad, got, total, s1, r1, s2, r2, s3, r3, mine, ssem, rsem, zs, zr, ls
):
    z = lax.axis_index("seq")
    me, c, f, s = ring_places()

    def device(ff, ss):
        return ff * (8 - 6 * c) + ss * (2 + 6 * c) + c

    partner = me + 1 - 2 * c
    f_right, f_left, f_far = lax.rem(f + 1, 4), lax.rem(f + 3, 4), lax.rem(f + 2, 4)
    s_right, s_left, s_far = lax.rem(s + 1, 4), lax.rem(s + 3, 4), lax.rem(s + 2, 4)
    right1, left1 = device(f_right, s), device(f_left, s)
    right2, left2 = device(f, s_right), device(f, s_left)
    barrier = greet((partner, right1, left1, right2, left2), me, z)
    half = lax.rem(z, 2)
    pl.semaphore_wait(barrier, 12)

    trade = remote(dk_ref.at[1 - half], pair, zs.at[14], zr.at[14], me, z + 1 - 2 * half)
    summed[NACT] = jnp.zeros((BLK, HEAD), BF)
    trade.wait_recv()
    summed[0:NACT] = (dk_ref[half] + pair[...]).astype(BF)
    for b in range(NBLK):
        pad[b] = summed[inv[b]]
    own = [local(pad.at[pl.ds(2 * z, 2)], got.at[z], ls.at[0])]
    spread, back = [], []
    for k in (1, 7, 2, 6, 3, 5, 4):
        t = lax.rem(z + k, 8)
        spread.append(remote(pad.at[pl.ds(2 * t, 2)], got.at[z], zs.at[k - 1], zr.at[k - 1], me, t))
    own.append(local(qg_ref.at[z], q_out.at[:, seq_rows(z), seq_lanes(z)], ls.at[1]))
    for k in (1, 7, 2, 6, 3, 5, 4):
        t = lax.rem(z + k, 8)
        back.append(
            remote(qg_ref.at[t], q_out.at[:, seq_rows(z), seq_lanes(z)], zs.at[6 + k], zr.at[6 + k], me, t)
        )
    own[0].wait()
    for copy in spread:
        copy.wait_recv()
    for j in range(8):
        lanes = slice(((j % 2) * KVH + j // 2) * HEAD, ((j % 2) * KVH + j // 2 + 1) * HEAD)
        kv2[0:128, lanes] = got[j, 0]
        kv2[128:256, lanes] = got[j, 1]

    def send(index, src, dst, dev, seq):
        return remote(src, dst, ssem.at[index], rsem.at[index], dev, seq)

    swap = send(0, kv2.at[0:256], kv2.at[256:512], partner, z)
    kvb_ref[...] = kv2[0:256, :]
    swap.wait()

    def product(ff, part):
        return jnp.dot(x_ref[ff, part * 320 : (part + 1) * 320, :], kv2[...], preferred_element_type=F32)

    s1[0] = product(f_far, 0).astype(BF)
    far_r = send(1, s1.at[0], r1.at[0], right1, z)
    s1[1] = product(f_far, 1).astype(BF)
    far_l = send(2, s1.at[1], r1.at[1], left1, z)
    s1[2] = product(f_right, 1).astype(BF)
    own_r = send(3, s1.at[2], r1.at[2], right1, z)
    s1[3] = product(f_left, 0).astype(BF)
    own_l = send(4, s1.at[3], r1.at[3], left1, z)
    total[0:2] = product(f_right, 0).reshape(2, 160, 1024)
    far_r.wait_recv()
    s1[4] = (total[0:2].reshape(320, 1024) + r1[0].astype(F32)).astype(BF)
    sum_r = send(5, s1.at[4], r1.at[4], right1, z)
    total[2:4] = product(f_left, 1).reshape(2, 160, 1024)
    far_l.wait_recv()
    s1[5] = (total[2:4].reshape(320, 1024) + r1[1].astype(F32)).astype(BF)
    sum_l = send(6, s1.at[5], r1.at[5], left1, z)
    total[0:2] = product(f, 0).reshape(2, 160, 1024)
    total[2:4] = product(f, 1).reshape(2, 160, 1024)
    own_r.wait_recv()
    own_l.wait_recv()
    total[0:2] += r1[3].astype(F32).reshape(2, 160, 1024)
    total[2:4] += r1[2].astype(F32).reshape(2, 160, 1024)
    sum_r.wait_recv()
    total[0:2] += r1[4].astype(F32).reshape(2, 160, 1024)
    sum_l.wait_recv()
    total[2:4] += r1[5].astype(F32).reshape(2, 160, 1024)

    s2[0] = total[s_far, 0:80, :].astype(BF)
    far_r2 = send(7, s2.at[0], r2.at[0], right2, z)
    s2[1] = total[s_far, 80:160, :].astype(BF)
    far_l2 = send(8, s2.at[1], r2.at[1], left2, z)
    s2[2] = total[s_right, 80:160, :].astype(BF)
    own_r2 = send(9, s2.at[2], r2.at[2], right2, z)
    s2[3] = total[s_left, 0:80, :].astype(BF)
    own_l2 = send(10, s2.at[3], r2.at[3], left2, z)
    far_r2.wait_recv()
    s2[4] = (total[s_right, 0:80, :] + r2[0].astype(F32)).astype(BF)
    sum_r2 = send(11, s2.at[4], r2.at[4], right2, z)
    far_l2.wait_recv()
    s2[5] = (total[s_left, 80:160, :] + r2[1].astype(F32)).astype(BF)
    sum_l2 = send(12, s2.at[5], r2.at[5], left2, z)
    own_r2.wait_recv()
    own_l2.wait_recv()
    sum_r2.wait_recv()
    top = total[s, 0:80, :] + r2[3].astype(F32) + r2[4].astype(F32)
    sum_l2.wait_recv()
    low = total[s, 80:160, :] + r2[2].astype(F32) + r2[5].astype(F32)
    for t in range(8):
        lanes = slice(t * 128, (t + 1) * 128)
        mine[t, 0:80, :] = top[:, lanes]
        mine[t, 80:160, :] = low[:, lanes]
        s3[t, 0:80, :] = top[:, lanes].astype(BF)
        s3[t, 80:160, :] = low[:, lanes].astype(BF)
    ends = []
    for k in range(1, 8):
        t = lax.rem(z + k, 8)
        ends.append(send(12 + k, s3.at[t], r3.at[k - 1], me, t))
    out = mine[z]
    for k in range(1, 8):
        ends[k - 1].wait_recv()
        out = out + r3[k - 1].astype(F32)
    out_ref[...] = out
    for copy in [far_r, far_l, own_r, own_l, sum_r, sum_l, far_r2, far_l2, own_r2, own_l2, sum_r2, sum_l2, trade] + ends + spread:
        copy.wait_send()
    own[1].wait()
    for copy in back:
        copy.wait()


def weight_gradient(inv, x, dk, qg):
    return pl.pallas_call(
        grad_kernel,
        out_shape=(
            jax.ShapeDtypeStruct((160, 128), F32),
            jax.ShapeDtypeStruct((256, 1024), BF),
            jax.ShapeDtypeStruct((2, BLK, 2560), BF),
        ),
        in_specs=[pl.BlockSpec(memory_space=pltpu.SMEM), VM, VM, ANY],
        out_specs=(VM, VM, ANY),
        scratch_shapes=[
            pltpu.VMEM((512, 1024), BF),
            pltpu.VMEM((NACT, BLK, HEAD), F32),
            pltpu.VMEM((NACT + 1, BLK, HEAD), BF),
            pltpu.VMEM((NBLK, BLK, HEAD), BF),
            pltpu.VMEM((8, 2, BLK, HEAD), BF),
            pltpu.VMEM((4, 160, 1024), F32),
            pltpu.VMEM((6, 320, 1024), BF),
            pltpu.VMEM((6, 320, 1024), BF),
            pltpu.VMEM((6, 80, 1024), BF),
            pltpu.VMEM((6, 80, 1024), BF),
            pltpu.VMEM((8, 160, 128), BF),
            pltpu.VMEM((7, 160, 128), BF),
            pltpu.VMEM((8, 160, 128), F32),
            pltpu.SemaphoreType.DMA((20,)),
            pltpu.SemaphoreType.DMA((20,)),
            pltpu.SemaphoreType.DMA((15,)),
            pltpu.SemaphoreType.DMA((15,)),
            pltpu.SemaphoreType.DMA((2,)),
        ],
        compiler_params=pltpu.CompilerParams(collective_id=0, has_side_effects=True),
        name="weight_gradient",
    )(inv, x, dk, qg)


def body(tokens, queries, cotangent, kv_weight, active):
    dp = lax.axis_index("dp")
    z = lax.axis_index("seq")
    core = lax.rem(dp, 2)
    x = tokens[0]
    x_t = x.T.reshape(4, 4, 2, 160, 256)

    def half_of(which):
        return jnp.where(which == 0, x_t[:, :, 0], x_t[:, :, 1].transpose(1, 0, 2, 3)).reshape(4, 640, 256)

    x_theirs = lax.ppermute(half_of(1 - core), "dp", [(i, i ^ 1) for i in range(32)])
    x_cat = jnp.concatenate([half_of(core), x_theirs], axis=2)
    act = jnp.concatenate([active[0], lax.rem(z, 2)[None].astype(jnp.int32)])
    same = active[0][None, :] == jnp.arange(NBLK, dtype=jnp.int32)[:, None]
    inv = NACT - jnp.sum(jnp.where(same, NACT - jnp.arange(NACT, dtype=jnp.int32)[None, :], 0), axis=1)

    queries, cotangent, x_cat = lax.optimization_barrier((queries, cotangent, x_cat))
    q_in, g_in, kv_in, weight = gather(
        queries.reshape(2, BLK, 2560), cotangent.reshape(2, BLK, 2560), kv_weight, x
    )
    rows = (NBLK, HALF, GRP * HEAD)
    qg, dkv = attention(act, q_in.reshape(rows), g_in.reshape(rows), kv_in.reshape(NBLK, BLK, 256))
    part, kv_back, q_back = weight_gradient(inv, x_cat, dkv, qg.reshape(8, 2, HALF, GRP * HEAD))
    token_grad = lax.dot_general(kv_back, weight.reshape(5120, 1024), NT, preferred_element_type=F32).astype(BF)
    return (q_back.reshape(1, 256, 2560), token_grad[None], part)


def solution(mesh):
    in_specs = (
        P("dp", "seq", None),
        P("dp", "seq", None),
        P("dp", "seq", None),
        P("dp", None),
        P("dp", None),
    )
    out_specs = (P("dp", "seq", None), P("dp", "seq", None), P("dp", "seq"))
    return jax.shard_map(body, mesh=mesh, in_specs=in_specs, out_specs=out_specs, check_vma=False)
```
